256 devices in a mesh: blk: 256 (over x, z, y, core).
Axes of the slice: x: 4, y: 4, z: 8, core: 2. Of those that a mesh axis runs over, the one named last changes fastest.
Arguments:
- diag_block: float32 [256, 512, 512], P('blk'), may hold values from -0.6 to 12.6, as said below
- near_blocks: float32 [256, 6, 512, 512], P('blk'), may hold values from -0.15 to 0.15
- far_coupling: float32 [256, 5, 256, 256], P('blk'), may hold values from -0.15 to 0.15
- leaf_basis: float32 [256, 512, 512], P('blk'), may hold values from -0.2 to 1.2
- parent_basis: float32 [65536, 1024], P('blk'), may hold values from -0.2 to 1.2
- near_index: int32 [256, 6], P('blk'), may hold values from 0 to 255, as said below
- far_index: int32 [256, 5], P('blk'), may hold values from 0 to 255, as said below
Outputs:
- leaf_factor: float32 [65536, 512], P('blk')
- parent_cholesky_factor: float32 [65536, 768], P('blk')
- parent_coupling: float32 [65536, 768], P('blk')
The draws below stay inside these ranges and needn't reach their ends.
Inputs may be any that keep to these rules, and one draw needn't show every extreme that they name: `near_index`: row i lists 6 different leaves, none equal to i, among the 12 leaves of parents i // 4 - 1, i // 4, i // 4 + 1 (modulo 64). `far_index`: row i lists the remaining 5 leaves of those parents: i, its near list and its far list name each of the 12 leaves once. `diag_block`: each block is symmetric.
All inputs are finite; a program needn't handle non-finite values.
Results may differ from the reference program's by a relative error of at most 0.0003.
Values sent between devices are 32-bit elements; how exact they have to be, the bound alone decides.
A program may use at most 192 MiB of HBM per device.

```python
import jax
import jax.numpy as jnp
from jax import lax

LEAF = 512
RANK = 256
NEAR = 6
GROUP = 4
BLOCKS = 256
PARENTS = 64
REDUN = 256
PAR = 1024
PRED = 768
FAR = 5


def draw_diag_block(key, part):
    random_portion = jax.random.uniform(key, (BLOCKS, LEAF, LEAF), jnp.float32, -0.3, 0.3)
    symmetric = 0.5 * (random_portion + jnp.swapaxes(random_portion, 1, 2))
    identity = jnp.eye(LEAF, dtype=jnp.float32)
    return symmetric + 12.0 * identity[None]


def basis_noise(key, shape, order):
    spread = 0.2 / order ** 0.5
    return jnp.clip(jax.random.normal(key, shape, jnp.float32) * spread, -4.0 * spread, 4.0 * spread)


def draw_leaf_basis(key, part):
    identity = jnp.eye(LEAF, dtype=jnp.float32)
    return identity[None] + basis_noise(key, (BLOCKS, LEAF, LEAF), LEAF)


def draw_parent_basis(key, part):
    identity = jnp.tile(jnp.eye(PAR, dtype=jnp.float32), (PARENTS, 1))
    return identity + basis_noise(key, (PARENTS * PAR, PAR), PAR)


def window_lists(key):
    row_keys = jax.random.split(jax.random.fold_in(key, 7), BLOCKS)
    shuffled = jax.vmap(lambda row_key: jax.random.permutation(row_key, 3 * GROUP - 1))(row_keys).astype(jnp.int32)
    leaf_ids = jnp.arange(BLOCKS, dtype=jnp.int32)[:, None]
    own_column = GROUP + leaf_ids % GROUP
    columns = shuffled + (shuffled >= own_column).astype(jnp.int32)
    parent = leaf_ids // GROUP
    return ((GROUP * (parent - 1) + columns) % BLOCKS).astype(jnp.int32)


def draw_near_index(key, part):
    return window_lists(key)[:, :NEAR]


def draw_far_index(key, part):
    return window_lists(key)[:, NEAR:]


def levels(key, shape, cuts, smallest, high):
    gain, own = 1.0, jax.random.fold_in(key, 6)
    for axis_at, blocks in cuts:
        draws = jnp.exp(jax.random.uniform(jax.random.fold_in(own, axis_at), (blocks,), jnp.float32, smallest / len(cuts), high / len(cuts)))
        gain = gain * jnp.repeat(draws, shape[axis_at] // blocks).reshape([-1 if axis == axis_at else 1 for axis in range(len(shape))])
    return gain


def noise(stream_key, dims, deviation, bound, shards=(), held_as=jnp.bfloat16):
    gain = levels(stream_key, dims, shards, -0.22, 0.18) if shards else 1.0
    drawn = jax.random.normal(stream_key, dims, jnp.float32) * deviation * gain
    return jnp.minimum(jnp.maximum(drawn, -bound), bound).astype(held_as)


def setup_inputs(seed: int = 0) -> dict:
    keys = jax.random.split(jax.random.key(seed), 8)
    diag_block = draw_diag_block(jax.random.fold_in(keys[7], 71), 0)
    near_blocks = noise(keys[1], (BLOCKS, NEAR, LEAF, LEAF), 0.025, 0.15, ((0, 256),), jnp.float32)
    far_coupling = noise(keys[2], (BLOCKS, FAR, RANK, RANK), 0.025, 0.15, ((0, 256),), jnp.float32)
    leaf_basis = draw_leaf_basis(jax.random.fold_in(keys[7], 71), 0)
    parent_basis = draw_parent_basis(jax.random.fold_in(keys[7], 71), 0)
    near_index = draw_near_index(jax.random.fold_in(keys[7], 71), 0)
    far_index = draw_far_index(jax.random.fold_in(keys[7], 71), 0)
    return {"diag_block": diag_block, "near_blocks": near_blocks, "far_coupling": far_coupling, "leaf_basis": leaf_basis, "parent_basis": parent_basis, "near_index": near_index, "far_index": far_index}


precise_mode = lax.Precision.HIGHEST

def matmul(left_side, right_side):
    return jnp.dot(left_side, right_side, precision=precise_mode)

def sym_cholesky(square):
    return jnp.linalg.cholesky(0.5 * (square + square.T))

def lower_solve(triangle, right_side):
    return lax.linalg.triangular_solve(triangle, right_side, left_side=True, lower=True)

def leaf_eliminate(diag_one, basis_one):
    transformed = matmul(matmul(basis_one.T, diag_one), basis_one)
    leaf_low = sym_cholesky(transformed[:REDUN, :REDUN])
    coupled = lower_solve(leaf_low, transformed[:REDUN, REDUN:])
    leaf_schur = transformed[REDUN:, REDUN:] - matmul(coupled.T, coupled)
    return (jnp.concatenate([leaf_low, coupled], axis=1), leaf_schur)

def reference(diag_block, near_blocks, far_coupling, leaf_basis, parent_basis, near_index, far_index):
    skel_all = leaf_basis[:, :, REDUN:]
    bases = parent_basis.reshape(PARENTS, PAR, PAR)
    prev_skel = jnp.roll(bases, 1, axis=0)[:, :, PRED:]
    next_skel = jnp.roll(bases, -1, axis=0)[:, :, PRED:]
    leaf_ids = jnp.arange(BLOCKS, dtype=jnp.int32).reshape(PARENTS, GROUP)
    columns = jnp.arange(3 * GROUP, dtype=jnp.int32)

    def per_parent(packed):
        diag_group, near_group, far_group, basis_group, near_ids, far_ids, own_ids, parent_q, prev_q, next_q = packed
        factors, schur_all = jax.vmap(leaf_eliminate)(diag_group, basis_group)
        skel_own = basis_group[:, :, REDUN:]
        skeleton_near_block = jnp.take(skel_all, near_ids, axis=0)
        left_side_product = jnp.einsum('gar,gmac->gmrc', skel_own, near_group, precision=precise_mode)
        near_summands = jnp.einsum('yeiv,yevf->yeif', left_side_product, skeleton_near_block, precision=precise_mode)
        start = GROUP * (own_ids[0] // GROUP - 1)
        near_hot = (((near_ids - start) % BLOCKS)[..., None] == columns).astype(jnp.float32)
        far_hot = (((far_ids - start) % BLOCKS)[..., None] == columns).astype(jnp.float32)
        self_hot = ((GROUP + own_ids % GROUP)[:, None] == columns).astype(jnp.float32)
        window_blocks = jnp.einsum('gmc,gmab->gcab', near_hot, near_summands, precision=precise_mode)
        window_blocks = window_blocks + jnp.einsum('gmc,gmab->gcab', far_hot, far_group, precision=precise_mode)
        window_blocks = window_blocks + self_hot[:, :, None, None] * schur_all[:, None]
        hfull = jnp.transpose(window_blocks, (0, 2, 1, 3)).reshape(PAR, 3 * PAR)
        c_self = matmul(parent_q.T, matmul(hfull[:, PAR:2 * PAR], parent_q))
        c_prev = matmul(parent_q.T, matmul(hfull[:, :PAR], prev_q))
        c_next = matmul(parent_q.T, matmul(hfull[:, 2 * PAR:], next_q))
        parent_low = sym_cholesky(c_self[:PRED, :PRED])
        parent_coupled = lower_solve(parent_low, c_self[:PRED, PRED:])
        parent_trans = lower_solve(parent_low, c_self[PRED:, :PRED].T)
        parent_schur = c_self[PRED:, PRED:] - matmul(parent_trans.T, parent_coupled)
        factor_all = jnp.concatenate([parent_low, parent_coupled.T], axis=0)
        edge_block = jnp.concatenate([c_self[:PRED, PRED:], parent_schur], axis=0)
        coupling_all = jnp.concatenate([c_prev, edge_block, c_next], axis=1)
        return (factors, factor_all, coupling_all)
    packed_inputs = (diag_block.reshape(PARENTS, GROUP, LEAF, LEAF), near_blocks.reshape(PARENTS, GROUP, NEAR, LEAF, LEAF), far_coupling.reshape(PARENTS, GROUP, FAR, RANK, RANK), leaf_basis.reshape(PARENTS, GROUP, LEAF, LEAF), near_index.reshape(PARENTS, GROUP, NEAR), far_index.reshape(PARENTS, GROUP, FAR), leaf_ids, bases, prev_skel, next_skel)
    factors, parent_factors, couplings = lax.map(per_parent, packed_inputs)
    return (factors.reshape(BLOCKS * REDUN, LEAF), parent_factors.reshape(PARENTS * PAR, PRED), couplings.reshape(PARENTS * PAR, 3 * RANK))
```

```python
import jax
import jax.numpy as jnp
from jax import lax
from jax.experimental import pallas as pl
from jax.experimental.pallas import tpu as pltpu
from jax.sharding import PartitionSpec as P

LEAF = 512
RANK = 256
NEAR = 6
GROUP = 4
REDUN = 256
PAR = 1024
PRED = 768
FAR = 5
TILE = 128
F32 = jnp.float32
BF16 = jnp.bfloat16
NN = (((1,), (0,)), ((), ()))
NT = (((1,), (1,)), ((), ()))
TN = (((0,), (0,)), ((), ()))


def split2(x):
    high = x.astype(BF16)
    return high, (x - high.astype(F32)).astype(BF16)


def dot_split(a, b, dims):
    (ah, al), (bh, bl) = a, b
    out = lax.dot_general(ah, bh, dims, preferred_element_type=F32)
    out += lax.dot_general(ah, bl, dims, preferred_element_type=F32)
    return out + lax.dot_general(al, bh, dims, preferred_element_type=F32)


def dot3(a, b, dims):
    return dot_split(split2(a), split2(b), dims)


def chol_tile(square):
    n, k = TILE, 32
    sub = lax.broadcasted_iota(jnp.int32, (k, n), 0)
    lane = lax.broadcasted_iota(jnp.int32, (k, n), 1)
    uppers, inverses = [], []
    rest, rest_inv = square, None
    for window in range(n // k):
        j0 = window * k
        rows = rest[:k]
        eye = (lane == sub + j0).astype(F32)
        inv = eye if rest_inv is None else rest_inv[:k] + eye
        cols = [jnp.broadcast_to(rows[:, j0 + c : j0 + c + 1], (k, n)) for c in range(k)]
        for c in range(k):
            base = c // 8 * 8
            height = k - base
            pivot = jnp.broadcast_to(cols[c][c - base : c - base + 1, :], (8, n))
            scale = lax.rsqrt(pivot)
            tall = jnp.concatenate([scale] * (height // 8), 0)
            low = jnp.where(sub[base:] > c, cols[c] * tall, 0.0)
            row_u = jnp.broadcast_to(rows[c - base : c - base + 1, :], (8, n)) * scale
            row_i = jnp.broadcast_to(inv[c - base : c - base + 1, :], (8, n)) * scale
            for e in range(c + 1, k):
                cols[e] = cols[e] - low * jnp.broadcast_to(low[e - base : e - base + 1, :], (height, n))
            row_u = jnp.concatenate([row_u] * (height // 8), 0)
            row_i = jnp.concatenate([row_i] * (height // 8), 0)
            rows = jnp.where(sub[base:] == c, row_u, rows - low * row_u)
            inv = jnp.where(sub[base:] == c, row_i, inv - low * row_i)
            if c % 8 == 7:
                uppers.append(rows[:8])
                inverses.append(inv[:8])
                rows, inv = rows[8:], inv[8:]
                cols = [col[8:] if col.shape[0] > 8 else col for col in cols]
        done = jnp.concatenate(uppers[-(k // 8) :], 0)
        done_inv = jnp.concatenate(inverses[-(k // 8) :], 0)
        done = jnp.where(lane >= sub + j0, done, 0.0)
        del uppers[-(k // 8) :]
        uppers.append(done)
        if j0 + k < n:
            both = jnp.concatenate([done, done_inv], axis=1)
            hi = both.astype(BF16)
            left = both - hi.astype(F32)
            mid = left.astype(BF16)
            lo = (left - mid.astype(F32)).astype(BF16)
            lhs = jnp.concatenate([hi[:, :n], hi[:, :n], mid[:, :n], hi[:, :n], lo[:, :n], mid[:, :n]], axis=0)
            rhs = jnp.concatenate([hi, mid, hi, lo, hi, mid], axis=0)
            update = lax.dot_general(lhs, rhs, TN, preferred_element_type=F32)[j0 + k :]
            rest = rest[k:] - update[:, :n]
            rest_inv = -update[:, n:] if rest_inv is None else rest_inv[k:] - update[:, n:]
    return jnp.concatenate(uppers, 0), jnp.concatenate(inverses, 0)


def leaf_kernel(diag_ref, basis_ref, out_ref, schur_ref):
    basis = split2(basis_ref[...])
    right = split2(dot_split(split2(diag_ref[...]), basis, NN))
    top = dot_split([q[:, :REDUN] for q in basis], right, TN)
    low_part = [q[:, REDUN:] for q in right]
    corner = dot_split([q[:, REDUN:] for q in basis], low_part, TN)
    upper, inverse = chol_tile(top[:TILE, :TILE])
    out_ref[:TILE, :TILE] = upper.T
    out_ref[:TILE, TILE:REDUN] = jnp.zeros((TILE, TILE), F32)
    across = dot3(inverse, top[:TILE, TILE:], NN)
    out_ref[TILE:, :TILE] = across[:, :TILE].T
    out_ref[:TILE, REDUN:] = across[:, TILE:]
    parts = split2(across)
    rest = top[TILE:, TILE:] - dot_split([q[:, :TILE] for q in parts], parts, TN)
    upper, inverse = chol_tile(rest[:, :TILE])
    out_ref[TILE:, TILE:REDUN] = upper.T
    across2 = dot3(inverse, rest[:, TILE:], NN)
    out_ref[TILE:, REDUN:] = across2
    coupled = split2(out_ref[:, REDUN:])
    schur_ref[...] = corner - dot_split(coupled, coupled, TN)


def window_kernel(index_ref, source_ref, basis_ref, near_ref, far_ref, schur_ref, skel_ref, rows_ref, prev_ref, next_ref, out_ref, blocks):
    skeleton = split2(basis_ref[:, REDUN:])

    def one_near(slot, carry):
        left = dot_split(skeleton, split2(near_ref[slot]), TN)
        blocks[slot] = dot3(left, skel_ref[index_ref[slot]], NN)
        return carry

    lax.fori_loop(0, NEAR, one_near, 0)
    for slot in range(FAR):
        blocks[NEAR + slot] = far_ref[slot]
    blocks[NEAR + FAR] = schur_ref[...]

    def term(column, rows):
        return dot3(blocks[source_ref[column]], rows, NN)

    for half in range(2):
        cols = slice(half * 512, half * 512 + 512)
        total = term(GROUP, rows_ref[0][:, cols])
        for child in range(1, GROUP):
            total += term(GROUP + child, rows_ref[child][:, cols])
        out_ref[:, cols] = total
    for base, ref, at in ((0, prev_ref, PAR), (2 * GROUP, next_ref, PAR + RANK)):
        total = term(base, ref[0])
        for child in range(1, GROUP):
            total += term(base + child, ref[child])
        out_ref[:, at : at + RANK] = total


def parent_kernel(member_ref, rows_ref, v_ref, factor_ref, couple_ref, basis_hi, basis_lo, v_hi, v_lo, c_ref, low_ref, low_hi, low_lo):
    member = member_ref[0]
    rows = PAR + RANK
    for child in range(GROUP):
        at = slice(child * RANK, child * RANK + RANK)
        basis_hi[at, :], basis_lo[at, :] = split2(rows_ref[child])
        v_hi[at, :], v_lo[at, :] = split2(v_ref[child])

    def piece(step, carry):
        at = pl.ds(pl.multiple_of(step * RANK, RANK), RANK)
        left = (basis_hi[:, at], basis_lo[:, at])
        c_ref[at, :] = dot_split(left, (v_hi[:, :PAR], v_lo[:, :PAR]), TN)
        return carry

    lax.fori_loop(0, GROUP, piece, 0)
    mine = pl.ds(pl.multiple_of(member * RANK, RANK), RANK)
    sides = dot_split((basis_hi[:, mine], basis_lo[:, mine]), (v_hi[:, PAR:], v_lo[:, PAR:]), TN)
    couple_ref[:, :RANK] = sides[:, :RANK]
    couple_ref[:, 2 * RANK :] = sides[:, RANK:]
    couple_ref[:, RANK : 2 * RANK] = c_ref[mine, PRED:]
    for j in range(PRED // TILE):
        cols = slice(j * TILE, j * TILE + TILE)
        for i in range(j, PRED // TILE):
            here = slice(i * TILE, i * TILE + TILE)
            low_ref[here, cols] = 0.5 * (c_ref[here, cols] + c_ref[cols, here].T)
            if i > j:
                low_ref[cols, here] = jnp.zeros((TILE, TILE), F32)
        for half in range(2):
            there = slice(PRED + half * TILE, PRED + half * TILE + TILE)
            low_ref[there, cols] = c_ref[cols, there].T
        low_ref[PAR:, cols] = c_ref[PRED:, cols]
    for b in range(PRED // TILE):
        cols = slice(b * TILE, b * TILE + TILE)
        strip = low_ref[b * TILE :, cols]
        if b:
            done = slice(0, b * TILE)
            left = (low_hi[b * TILE :, done], low_lo[b * TILE :, done])
            strip = strip - dot_split(left, (left[0][:TILE], left[1][:TILE]), NT)
        upper, inverse = chol_tile(strip[:TILE])
        low_ref[cols, cols] = upper.T
        below = dot3(strip[TILE:], inverse, NT)
        low_ref[(b + 1) * TILE :, cols] = below
        low_hi[(b + 1) * TILE :, cols], low_lo[(b + 1) * TILE :, cols] = split2(below)
    factor_ref[...] = low_ref[mine, :]

    @pl.when(member == GROUP - 1)
    def _():
        left = (low_hi[PAR:, :], low_lo[PAR:, :])
        right = (low_hi[PRED:PAR, :], low_lo[PRED:PAR, :])
        couple_ref[:, RANK : 2 * RANK] = c_ref[PRED:, PRED:] - dot_split(left, right, NT)


def passed_along(value, axis, steps):
    count = lax.axis_size(axis)
    pairs = [(source, (source + steps) % count) for source in range(count)]
    return lax.ppermute(value, axis, pairs)


def split_close(vector):
    return (vector[: LEAF * RANK].reshape(LEAF, RANK), vector[LEAF * RANK :].reshape(RANK, PAR))


def split_far(vector):
    return (vector[: LEAF * RANK].reshape(LEAF, RANK), vector[LEAF * RANK :].reshape(RANK, RANK))


def shape(*dims):
    return jax.ShapeDtypeStruct(dims, F32)


def vmem(count):
    return [pl.BlockSpec(memory_space=pltpu.VMEM)] * count


SMEM = pl.BlockSpec(memory_space=pltpu.SMEM)


def on_device(diag_block, near_blocks, far_coupling, leaf_basis, parent_basis, near_index, far_index):
    blocks = lax.axis_size("blk")
    myself = lax.axis_index("blk")
    member = myself % GROUP
    max_offset = 2 * GROUP - 1
    own_basis = leaf_basis[0]
    skeleton = own_basis[:, REDUN:]
    close_load = jnp.concatenate([skeleton.reshape(-1), parent_basis.reshape(-1)])
    far_load = jnp.concatenate([skeleton.reshape(-1), parent_basis[:, PRED:].reshape(-1)])
    received = {0: close_load}
    for offset in range(-max_offset, max_offset + 1):
        if 0 < abs(offset) < GROUP:
            received[offset] = passed_along(close_load, "blk", -offset)
        elif abs(offset) >= GROUP:
            received[offset] = passed_along(far_load, "blk", -offset)
    skel_list = []
    qskel_list = []
    qfull_list = []
    for offset in range(-max_offset, max_offset + 1):
        if abs(offset) < GROUP:
            skel_part, row_block = split_close(received[offset])
            qfull_list.append(row_block)
            qskel_list.append(row_block[:, PRED:])
        else:
            skel_part, row_block = split_far(received[offset])
            qskel_list.append(row_block)
        skel_list.append(skel_part)
    skel_stack = jnp.stack(skel_list)
    qskel_stack = jnp.stack(qskel_list)
    complete_basis_stack = jnp.stack(qfull_list)

    leaf_out, leaf_schur = pl.pallas_call(
        leaf_kernel,
        out_shape=(shape(REDUN, LEAF), shape(RANK, RANK)),
        in_specs=vmem(2),
        out_specs=tuple(vmem(2)),
        name="leaf",
        cost_estimate=pl.CostEstimate(flops=2 * 10**9, bytes_accessed=3 * 2**20, transcendentals=0),
    )(diag_block[0], own_basis)

    half_count = blocks // 2
    near_offset = (near_index[0] - myself + half_count) % blocks - half_count
    far_offset = (far_index[0] - myself + half_count) % blocks - half_count
    columns = jnp.arange(3 * GROUP, dtype=jnp.int32)
    near_slots = jnp.arange(NEAR, dtype=jnp.int32)
    far_slots = NEAR + jnp.arange(FAR, dtype=jnp.int32)
    near_match = ((near_offset + GROUP + member)[:, None] == columns).astype(jnp.int32)
    far_match = ((far_offset + GROUP + member)[:, None] == columns).astype(jnp.int32)
    self_match = (columns == GROUP + member).astype(jnp.int32)
    source = (
        jnp.sum(near_match * near_slots[:, None], axis=0)
        + jnp.sum(far_match * far_slots[:, None], axis=0)
        + self_match * (NEAR + FAR)
    )
    children = jnp.arange(GROUP, dtype=jnp.int32)
    prev_rows = jnp.take(qskel_stack, children - GROUP - member + max_offset, axis=0)
    own_rows = jnp.take(complete_basis_stack, children - member + GROUP - 1, axis=0)
    next_rows = jnp.take(qskel_stack, children + GROUP - member + max_offset, axis=0)

    joined = pl.pallas_call(
        window_kernel,
        out_shape=shape(RANK, PAR + 2 * RANK),
        in_specs=[SMEM, SMEM] + vmem(8),
        out_specs=vmem(1)[0],
        scratch_shapes=[pltpu.VMEM((NEAR + FAR + 1, RANK, RANK), F32)],
        name="window",
    )(near_offset + max_offset, source, own_basis, near_blocks[0], far_coupling[0], leaf_schur, skel_stack, own_rows, prev_rows, next_rows)

    distances = list(range(1, GROUP)) + list(range(1 - GROUP, 0))
    gathered = {0: joined}
    for distance in distances:
        gathered[distance] = passed_along(joined, "blk", distance)
    stacked = jnp.stack([gathered[distance] for distance in range(1 - GROUP, GROUP)])
    all_v = jnp.take(stacked, member - children + GROUP - 1, axis=0)

    factor_rows, coupling_rows = pl.pallas_call(
        parent_kernel,
        out_shape=(shape(RANK, PRED), shape(RANK, PRED)),
        in_specs=[SMEM] + vmem(2),
        out_specs=tuple(vmem(2)),
        scratch_shapes=[
            pltpu.VMEM((PAR, PAR), BF16),
            pltpu.VMEM((PAR, PAR), BF16),
            pltpu.VMEM((PAR, PAR + 2 * RANK), BF16),
            pltpu.VMEM((PAR, PAR + 2 * RANK), BF16),
            pltpu.VMEM((PAR, PAR), F32),
            pltpu.VMEM((PAR + RANK, PRED), F32),
            pltpu.VMEM((PAR + RANK, PRED), BF16),
            pltpu.VMEM((PAR + RANK, PRED), BF16),
        ],
        name="parent",
    )(member[None], own_rows, all_v)
    return (leaf_out, factor_rows, coupling_rows)


def solution(mesh):
    placed = (
        P("blk", None, None),
        P("blk", None, None, None),
        P("blk", None, None, None),
        P("blk", None, None),
        P("blk", None),
        P("blk", None),
        P("blk", None),
    )
    return jax.shard_map(
        on_device,
        mesh=mesh,
        in_specs=placed,
        out_specs=(P("blk", None), P("blk", None), P("blk", None)),
        check_vma=False,
    )
```

```python
import jax
import jax.numpy as jnp
from jax import lax
from jax.experimental import pallas as pl
from jax.experimental.pallas import tpu as pltpu
from jax.sharding import PartitionSpec as P

LEAF = 512
RANK = 256
NEAR = 6
GROUP = 4
REDUN = 256
PAR = 1024
PRED = 768
FAR = 5
TILE = 128
F32 = jnp.float32
BF16 = jnp.bfloat16
NN = (((1,), (0,)), ((), ()))
NT = (((1,), (1,)), ((), ()))
TN = (((0,), (0,)), ((), ()))
MESH = pl.DeviceIdType.MESH


def split2(x):
    high = x.astype(BF16)
    return high, (x - high.astype(F32)).astype(BF16)


def dot_split(a, b, dims):
    (ah, al), (bh, bl) = a, b
    out = lax.dot_general(ah, bh, dims, preferred_element_type=F32)
    out += lax.dot_general(ah, bl, dims, preferred_element_type=F32)
    return out + lax.dot_general(al, bh, dims, preferred_element_type=F32)


def dot3(a, b, dims):
    return dot_split(split2(a), split2(b), dims)


def chol_tile(square):
    n, k = TILE, 32
    sub = lax.broadcasted_iota(jnp.int32, (k, n), 0)
    lane = lax.broadcasted_iota(jnp.int32, (k, n), 1)
    uppers, inverses = [], []
    rest, rest_inv = square, None
    for window in range(n // k):
        j0 = window * k
        rows = rest[:k]
        eye = (lane == sub + j0).astype(F32)
        inv = eye if rest_inv is None else rest_inv[:k] + eye
        cols = [jnp.broadcast_to(rows[:, j0 + c : j0 + c + 1], (k, n)) for c in range(k)]
        for c in range(k):
            base = c // 8 * 8
            height = k - base
            pivot = jnp.broadcast_to(cols[c][c - base : c - base + 1, :], (8, n))
            scale = lax.rsqrt(pivot)
            tall = jnp.concatenate([scale] * (height // 8), 0)
            low = jnp.where(sub[base:] > c, cols[c] * tall, 0.0)
            row_u = jnp.broadcast_to(rows[c - base : c - base + 1, :], (8, n)) * scale
            row_i = jnp.broadcast_to(inv[c - base : c - base + 1, :], (8, n)) * scale
            for e in range(c + 1, k):
                cols[e] = cols[e] - low * jnp.broadcast_to(low[e - base : e - base + 1, :], (height, n))
            row_u = jnp.concatenate([row_u] * (height // 8), 0)
            row_i = jnp.concatenate([row_i] * (height // 8), 0)
            rows = jnp.where(sub[base:] == c, row_u, rows - low * row_u)
            inv = jnp.where(sub[base:] == c, row_i, inv - low * row_i)
            if c % 8 == 7:
                uppers.append(rows[:8])
                inverses.append(inv[:8])
                rows, inv = rows[8:], inv[8:]
                cols = [col[8:] if col.shape[0] > 8 else col for col in cols]
        done = jnp.concatenate(uppers[-(k // 8) :], 0)
        done_inv = jnp.concatenate(inverses[-(k // 8) :], 0)
        done = jnp.where(lane >= sub + j0, done, 0.0)
        del uppers[-(k // 8) :]
        uppers.append(done)
        if j0 + k < n:
            both = jnp.concatenate([done, done_inv], axis=1)
            hi = both.astype(BF16)
            left = both - hi.astype(F32)
            mid = left.astype(BF16)
            lo = (left - mid.astype(F32)).astype(BF16)
            lhs = jnp.concatenate([hi[:, :n], hi[:, :n], mid[:, :n], hi[:, :n], lo[:, :n], mid[:, :n]], axis=0)
            rhs = jnp.concatenate([hi, mid, hi, lo, hi, mid], axis=0)
            update = lax.dot_general(lhs, rhs, TN, preferred_element_type=F32)[j0 + k :]
            rest = rest[k:] - update[:, :n]
            rest_inv = -update[:, n:] if rest_inv is None else rest_inv[k:] - update[:, n:]
    return jnp.concatenate(uppers, 0), jnp.concatenate(inverses, 0)


def leaf_kernel(diag_ref, basis_ref, out_ref, schur_ref):
    basis = split2(basis_ref[...])
    right = split2(dot_split(split2(diag_ref[...]), basis, NN))
    top = dot_split([q[:, :REDUN] for q in basis], right, TN)
    low_part = [q[:, REDUN:] for q in right]
    corner = dot_split([q[:, REDUN:] for q in basis], low_part, TN)
    upper, inverse = chol_tile(top[:TILE, :TILE])
    out_ref[:TILE, :TILE] = upper.T
    out_ref[:TILE, TILE:REDUN] = jnp.zeros((TILE, TILE), F32)
    across = dot3(inverse, top[:TILE, TILE:], NN)
    out_ref[TILE:, :TILE] = across[:, :TILE].T
    out_ref[:TILE, REDUN:] = across[:, TILE:]
    parts = split2(across)
    rest = top[TILE:, TILE:] - dot_split([q[:, :TILE] for q in parts], parts, TN)
    upper, inverse = chol_tile(rest[:, :TILE])
    out_ref[TILE:, TILE:REDUN] = upper.T
    across2 = dot3(inverse, rest[:, TILE:], NN)
    out_ref[TILE:, REDUN:] = across2
    coupled = split2(out_ref[:, REDUN:])
    schur_ref[...] = corner - dot_split(coupled, coupled, TN)


def exchange_kernel(kind_ref, near_at_ref, far_at_ref, basis_ref, near_ref, far_ref, schur_ref, parent_ref, rows_ref, v_ref, skel, sides, near, far, left_hi, left_lo, h_hi, h_lo, local_sem, send_sem, recv_sem):
    me = lax.axis_index("blk")
    count = lax.axis_size("blk")
    core = lax.rem(me, 2)
    member = lax.rem(me, GROUP)
    y = lax.rem(lax.div(me, 2), 4)
    upper = lax.div(y, 2)
    other = lax.rem(member + 2, GROUP)
    partner = me + 1 - 2 * core
    sibling = me + 2 - 4 * lax.rem(y, 2)
    across = me + 2 * (3 - 2 * y)
    step = 8 - 16 * upper
    onward = lax.rem(me + step + count, count)
    behind = lax.rem(me - step + count, count)
    near_side, far_side = 2 - 2 * upper, 2 * upper

    def rows_of(child):
        return pl.ds(pl.multiple_of(child * RANK, RANK), RANK)

    mine = rows_of(member)
    left_cols, skel_cols = pl.ds(0, PRED), pl.ds(PRED, RANK)
    local = [
        pltpu.make_async_copy(basis_ref.at[:, pl.ds(REDUN, RANK)], skel.at[1, member], local_sem.at[0]),
        pltpu.make_async_copy(near_ref, near, local_sem.at[1]),
        pltpu.make_async_copy(parent_ref, rows_ref.at[mine, :], local_sem.at[2]),
        pltpu.make_async_copy(far_ref, far, local_sem.at[3]),
    ]
    for copy in local:
        copy.start()

    barrier = pltpu.get_barrier_semaphore()
    for device in (partner, sibling, across, onward, behind):
        pl.semaphore_signal(barrier, inc=1, device_id=(device,), device_id_type=MESH)
    pl.semaphore_wait(barrier, 5)

    started = []

    def send(src, dst, device):
        at = len(started)
        copy = pltpu.make_async_remote_copy(
            src_ref=src, dst_ref=dst, send_sem=send_sem.at[at], recv_sem=recv_sem.at[at], device_id=(device,), device_id_type=MESH
        )
        copy.start()
        started.append(copy)
        return copy

    def send_same(ref, device):
        return send(ref, ref, device)

    own_skel = basis_ref.at[:, pl.ds(REDUN, RANK)]
    own_side = parent_ref.at[:, skel_cols]
    sib_s = send(own_skel, skel.at[1, member], sibling)
    cross_s = send(own_skel, skel.at[far_side, member], across)
    pair_s = send(own_skel, skel.at[1, member], partner)
    sib_p = send(own_side, rows_ref.at[mine, skel_cols], sibling)
    cross_p = send(own_side, sides.at[upper, mine, :], across)
    pair_p = send(parent_ref, rows_ref.at[mine, :], partner)
    sib_r = send(parent_ref.at[:, left_cols], rows_ref.at[mine, left_cols], sibling)

    local[0].wait()
    local[1].wait()
    own = split2(skel[1, member].T)

    def one_near(slot, carry):
        left_hi[slot], left_lo[slot] = split2(dot_split(own, split2(near[slot]), NN))
        return carry

    lax.fori_loop(0, NEAR, one_near, 0)
    theirs = rows_of(other)
    sib_s.wait_recv()
    relay_s = send(skel.at[1, other], skel.at[far_side, other], across)
    pair_sib_s = send_same(skel.at[1, other], partner)
    cross_s.wait_recv()
    on_s = send(skel.at[near_side, other], skel.at[far_side, other], onward)
    pair_cross_s = send_same(skel.at[near_side, other], partner)
    sib_p.wait_recv()
    relay_p = send(rows_ref.at[theirs, skel_cols], sides.at[upper, theirs, :], across)
    cross_p.wait_recv()
    on_p = send(sides.at[1 - upper, theirs, :], sides.at[upper, theirs, :], onward)
    pair_cross_p = send_same(sides.at[1 - upper, theirs, :], partner)
    relay_s.wait_recv()
    on_relay_s = send(skel.at[near_side, member], skel.at[far_side, member], onward)
    pair_relay_s = send_same(skel.at[near_side, member], partner)
    on_s.wait_recv()
    pair_on_s = send_same(skel.at[far_side, other], partner)
    relay_p.wait_recv()
    on_relay_p = send(sides.at[1 - upper, mine, :], sides.at[upper, mine, :], onward)
    pair_relay_p = send_same(sides.at[1 - upper, mine, :], partner)
    on_p.wait_recv()
    pair_on_p = send_same(sides.at[upper, theirs, :], partner)
    sib_r.wait_recv()
    pair_sib_p = send_same(rows_ref.at[theirs, :], partner)
    local[2].wait()
    local[3].wait()

    def fill(side):
        def one(child, carry):
            column = side * GROUP + child
            left = (left_hi[near_at_ref[column]], left_lo[near_at_ref[column]])
            block = dot_split(left, split2(skel[side, child]), NN)
            block = jnp.where(kind_ref[column] == 1, block, far[far_at_ref[column]])
            block = jnp.where((column == GROUP + member), schur_ref[...], block)
            at = rows_of(child)
            h_hi[:, at], h_lo[:, at] = split2(block)
            return carry

        lax.fori_loop(0, GROUP, one, 0)
        return h_hi[...], h_lo[...]

    pair_s.wait_recv()
    pair_sib_s.wait_recv()
    pair_p.wait_recv()
    h_own = fill(1)
    pair_sib_p.wait_recv()
    v_pairs, v_sibs = [], []
    for part in range(2):
        cols = pl.ds(part * 512, 512)
        v_ref[mine, cols] = dot_split(h_own, split2(rows_ref[:, cols]), NN)
        v_sibs.append(send_same(v_ref.at[mine, cols], sibling))
        v_pairs.append(send_same(v_ref.at[mine, cols], partner))
    pair_cross_s.wait_recv()
    pair_cross_p.wait_recv()
    pair_relay_s.wait_recv()
    pair_relay_p.wait_recv()

    def side_product(side, at):
        v_ref[mine, pl.ds(PAR + pl.multiple_of(at * RANK, RANK), RANK)] = dot_split(fill(side), split2(sides[at]), NN)

    side_product(near_side, 1 - upper)
    on_relay_s.wait_recv()
    pair_on_relay_s = send_same(skel.at[far_side, member], partner)
    on_relay_p.wait_recv()
    pair_on_relay_p = send_same(sides.at[upper, mine, :], partner)
    pair_on_s.wait_recv()
    pair_on_p.wait_recv()
    pair_on_relay_s.wait_recv()
    pair_on_relay_p.wait_recv()
    side_product(far_side, upper)
    cols = pl.ds(PAR, 2 * RANK)
    v_sibs.append(send_same(v_ref.at[mine, cols], sibling))
    v_pairs.append(send_same(v_ref.at[mine, cols], partner))
    passed = []
    for part in range(3):
        v_sibs[part].wait_recv()
        passed.append(send_same(v_ref.at[theirs, pl.ds(part * 512, 512)], partner))
    for copy in v_pairs + passed:
        copy.wait_recv()
    for copy in started:
        copy.wait_send()


COPIES = 32


def parent_kernel(member_ref, rows_ref, v_ref, factor_ref, couple_ref, basis_hi, basis_lo, v_hi, v_lo, c_ref, low_ref, low_hi, low_lo):
    member = member_ref[0]
    rows = PAR + RANK
    for child in range(GROUP):
        at = slice(child * RANK, child * RANK + RANK)
        basis_hi[at, :], basis_lo[at, :] = split2(rows_ref[at, :])
        v_hi[at, :], v_lo[at, :] = split2(v_ref[at, :])

    def piece(step, carry):
        at = pl.ds(pl.multiple_of(step * RANK, RANK), RANK)
        left = (basis_hi[:, at], basis_lo[:, at])
        c_ref[at, :] = dot_split(left, (v_hi[:, :PAR], v_lo[:, :PAR]), TN)
        return carry

    lax.fori_loop(0, GROUP, piece, 0)
    mine = pl.ds(pl.multiple_of(member * RANK, RANK), RANK)
    sides = dot_split((basis_hi[:, mine], basis_lo[:, mine]), (v_hi[:, PAR:], v_lo[:, PAR:]), TN)
    couple_ref[:, :RANK] = sides[:, :RANK]
    couple_ref[:, 2 * RANK :] = sides[:, RANK:]
    couple_ref[:, RANK : 2 * RANK] = c_ref[mine, PRED:]
    for j in range(PRED // TILE):
        cols = slice(j * TILE, j * TILE + TILE)
        for i in range(j, PRED // TILE):
            here = slice(i * TILE, i * TILE + TILE)
            low_ref[here, cols] = 0.5 * (c_ref[here, cols] + c_ref[cols, here].T)
            if i > j:
                low_ref[cols, here] = jnp.zeros((TILE, TILE), F32)
        for half in range(2):
            there = slice(PRED + half * TILE, PRED + half * TILE + TILE)
            low_ref[there, cols] = c_ref[cols, there].T
        low_ref[PAR:, cols] = c_ref[PRED:, cols]
    for b in range(PRED // TILE):
        cols = slice(b * TILE, b * TILE + TILE)
        strip = low_ref[b * TILE :, cols]
        if b:
            done = slice(0, b * TILE)
            left = (low_hi[b * TILE :, done], low_lo[b * TILE :, done])
            strip = strip - dot_split(left, (left[0][:TILE], left[1][:TILE]), NT)
        upper, inverse = chol_tile(strip[:TILE])
        low_ref[cols, cols] = upper.T
        below = dot3(strip[TILE:], inverse, NT)
        low_ref[(b + 1) * TILE :, cols] = below
        low_hi[(b + 1) * TILE :, cols], low_lo[(b + 1) * TILE :, cols] = split2(below)
    factor_ref[...] = low_ref[mine, :]

    @pl.when(member == GROUP - 1)
    def _():
        left = (low_hi[PAR:, :], low_lo[PAR:, :])
        right = (low_hi[PRED:PAR, :], low_lo[PRED:PAR, :])
        couple_ref[:, RANK : 2 * RANK] = c_ref[PRED:, PRED:] - dot_split(left, right, NT)


def shape(*dims):
    return jax.ShapeDtypeStruct(dims, F32)


def vmem(count):
    return [pl.BlockSpec(memory_space=pltpu.VMEM)] * count


SMEM = pl.BlockSpec(memory_space=pltpu.SMEM)


def on_device(diag_block, near_blocks, far_coupling, leaf_basis, parent_basis, near_index, far_index):
    blocks = lax.axis_size("blk")
    myself = lax.axis_index("blk")
    member = myself % GROUP
    own_basis = leaf_basis[0]
    leaf_out, leaf_schur = pl.pallas_call(
        leaf_kernel,
        out_shape=(shape(REDUN, LEAF), shape(RANK, RANK)),
        in_specs=vmem(2),
        out_specs=tuple(vmem(2)),
        name="leaf",
        cost_estimate=pl.CostEstimate(flops=2 * 10**9, bytes_accessed=3 * 2**20, transcendentals=0),
    )(diag_block[0], own_basis)

    start = GROUP * (myself // GROUP - 1)
    columns = jnp.arange(3 * GROUP, dtype=jnp.int32)
    near_match = ((near_index[0] - start + blocks) % blocks)[:, None] == columns
    far_match = ((far_index[0] - start + blocks) % blocks)[:, None] == columns
    near_at = jnp.sum(near_match * jnp.arange(NEAR, dtype=jnp.int32)[:, None], axis=0)
    far_at = jnp.sum(far_match * jnp.arange(FAR, dtype=jnp.int32)[:, None], axis=0)
    kind = jnp.sum(near_match.astype(jnp.int32), axis=0)
    anywhere = [pl.BlockSpec(memory_space=pl.ANY)]
    all_rows, all_v = pl.pallas_call(
        exchange_kernel,
        out_shape=(shape(PAR, PAR), shape(PAR, PAR + 2 * RANK)),
        in_specs=[SMEM] * 3 + anywhere * 3 + vmem(1) + anywhere,
        out_specs=tuple(vmem(2)),
        scratch_shapes=[
            pltpu.VMEM((3, GROUP, LEAF, RANK), F32),
            pltpu.VMEM((2, PAR, RANK), F32),
            pltpu.VMEM((NEAR, LEAF, LEAF), F32),
            pltpu.VMEM((FAR, RANK, RANK), F32),
            pltpu.VMEM((NEAR, RANK, LEAF), BF16),
            pltpu.VMEM((NEAR, RANK, LEAF), BF16),
            pltpu.VMEM((RANK, PAR), BF16),
            pltpu.VMEM((RANK, PAR), BF16),
            pltpu.SemaphoreType.DMA((4,)),
            pltpu.SemaphoreType.DMA((COPIES,)),
            pltpu.SemaphoreType.DMA((COPIES,)),
        ],
        compiler_params=pltpu.CompilerParams(collective_id=0, has_side_effects=True),
        name="exchange",
    )(kind, near_at, far_at, own_basis, near_blocks[0], far_coupling[0], leaf_schur, parent_basis)

    factor_rows, coupling_rows = pl.pallas_call(
        parent_kernel,
        out_shape=(shape(RANK, PRED), shape(RANK, PRED)),
        in_specs=[SMEM] + vmem(2),
        out_specs=tuple(vmem(2)),
        scratch_shapes=[
            pltpu.VMEM((PAR, PAR), BF16),
            pltpu.VMEM((PAR, PAR), BF16),
            pltpu.VMEM((PAR, PAR + 2 * RANK), BF16),
            pltpu.VMEM((PAR, PAR + 2 * RANK), BF16),
            pltpu.VMEM((PAR, PAR), F32),
            pltpu.VMEM((PAR + RANK, PRED), F32),
            pltpu.VMEM((PAR + RANK, PRED), BF16),
            pltpu.VMEM((PAR + RANK, PRED), BF16),
        ],
        name="parent",
    )(member[None], all_rows, all_v)
    return (leaf_out, factor_rows, coupling_rows)


def solution(mesh):
    placed = (
        P("blk", None, None),
        P("blk", None, None, None),
        P("blk", None, None, None),
        P("blk", None, None),
        P("blk", None),
        P("blk", None),
        P("blk", None),
    )
    return jax.shard_map(
        on_device,
        mesh=mesh,
        in_specs=placed,
        out_specs=(P("blk", None), P("blk", None), P("blk", None)),
        check_vma=False,
    )
```
